256 devices in a mesh: rows: 128 (over z_hi, y, x, core), feat: 2 (over z_lo).
Axes of the slice: x: 4, y: 4, z: 8 (z_hi: 4, z_lo: 2; z = z_hi * 2 + z_lo), core: 2. Of those that a mesh axis runs over, the one named last changes fastest.
Arguments:
- features: bfloat16 [98304, 8192], P('rows', 'feat'), may hold values from -400 to 400
- group_index_list: int32 [98304], P('rows'), may hold values from 0 to 4095
- threshold_codes: int32 [98304], P('rows'), may hold values from 0 to 3
Outputs:
- counts: float32 [2, 98304], P(None, 'rows')
The draws below stay inside these ranges and needn't reach their ends.
All inputs are finite; a program needn't handle non-finite values.
Results may differ from the reference program's by a relative error of at most 0.00058.
The reference program's roundings to bfloat16 on the way count: a program that leaves them out, or rounds other values in their place, can miss the bound.
Values may be sent and summed in bfloat16 or wider, within the bound.
A program may use at most 64 MiB of HBM per device.

```python
import math
import jax
import jax.numpy as jnp
from jax import lax

F = 8192
ROWS_DEV = 768
MEET = 3
GROUPS_BLOCK = 32
ROWS = 98304


def group_labels(key):
    blocks = ROWS // ROWS_DEV
    base_key = jax.random.fold_in(key, 11)
    key_ahead, key_member = jax.random.split(base_key)
    row_index = jnp.arange(ROWS, dtype=jnp.int32)
    block_of_row = row_index // ROWS_DEV
    forward_block_count = jax.random.randint(key_ahead, (ROWS,), 0, MEET + 1, dtype=jnp.int32)
    member = jax.random.randint(key_member, (ROWS,), 0, GROUPS_BLOCK, dtype=jnp.int32)
    labels = (block_of_row + forward_block_count) % blocks * GROUPS_BLOCK + member
    maximum_score = blocks * GROUPS_BLOCK - 1
    labels = jnp.where(row_index == ROWS - 1, maximum_score, labels)
    labels = jnp.where(row_index == 0, 0, labels)
    return labels.astype(jnp.int32)


def draw_group_index_list(key, part):
    return group_labels(key)


def draw_features(key, part):
    blocks = ROWS // ROWS_DEV
    labels = group_labels(key)
    key_mix, key_private, key_rowscale, key_colscale, key_dirs = jax.random.split(jax.random.fold_in(key, 23), 5)
    directions = jax.random.normal(key_dirs, (blocks * GROUPS_BLOCK // 2, F), jnp.float32)
    mixing = jax.random.uniform(key_mix, (ROWS, 1), jnp.float32, 0.45, 0.95)
    private = jax.random.normal(key_private, (ROWS, F), jnp.float32)
    row_scale = jnp.exp(jax.random.uniform(key_rowscale, (ROWS, 1), jnp.float32, 0.0, math.log(10.0)))
    col_scale = jnp.exp(jax.random.uniform(key_colscale, (1, F), jnp.float32, 0.0, math.log(10.0)))
    values = mixing * directions[labels // 2] + jnp.sqrt(1.0 - mixing * mixing) * private
    values = jnp.clip(values * row_scale * col_scale, -400.0, 400.0)
    values = values.at[ROWS - 1, 0].set(400.0)
    values = values.at[ROWS - 1, 1].set(-400.0)
    return values.astype(jnp.bfloat16)


def place_ends(drawn, key, smallest, largest):
    index_at = [jax.random.randint(jax.random.fold_in(key, axis), (), 0, length) for axis, length in enumerate(drawn.shape)]
    widest = drawn.shape.index(max(drawn.shape))
    neighbour = index_at[:widest] + [(index_at[widest] + 1) % drawn.shape[widest]] + index_at[widest + 1:]
    return drawn.at[tuple(index_at)].set(smallest).at[tuple(neighbour)].set(largest)


def setup_inputs(seed: int = 0) -> dict:
    seeds = jax.random.split(jax.random.key(seed), 4)
    features = draw_features(jax.random.fold_in(seeds[3], 71), 0)
    group_index_list = draw_group_index_list(jax.random.fold_in(seeds[3], 71), 0)
    threshold_codes = place_ends(jax.random.randint(seeds[2], (ROWS,), 0, 4), jax.random.fold_in(seeds[2], 1), 0, 3).astype(jnp.int32)
    return dict(features=features, group_index_list=group_index_list, threshold_codes=threshold_codes)


SOFTNESS_FACTOR = 0.02

def count_rows(score_matrix, level_codes, own_groups, other_groups):
    cutoff_levels = 0.2 + 0.15 * level_codes.astype(jnp.float32)
    weight_factors = jax.nn.sigmoid((score_matrix - cutoff_levels[:, None]) / SOFTNESS_FACTOR)
    same_group = own_groups[:, None] == other_groups[None, :]
    matched = lax.optimization_barrier(jnp.sum(jnp.where(same_group, weight_factors, 0.0), axis=1))
    overall = lax.optimization_barrier(jnp.sum(weight_factors, axis=1))
    return jnp.stack([matched, overall - matched])

def count_columns(score_matrix, level_codes, own_groups, other_groups):
    cutoff_levels = 0.2 + 0.15 * level_codes.astype(jnp.float32)
    weight_factors = jax.nn.sigmoid((score_matrix - cutoff_levels[None, :]) / SOFTNESS_FACTOR)
    same_group = other_groups[:, None] == own_groups[None, :]
    matched = lax.optimization_barrier(jnp.sum(jnp.where(same_group, weight_factors, 0.0), axis=0))
    overall = lax.optimization_barrier(jnp.sum(weight_factors, axis=0))
    return jnp.stack([matched, overall - matched])

def unit_rows(features):
    widened = features.astype(jnp.float32)
    squares = lax.optimization_barrier(jnp.sum(widened * widened, axis=1))
    inverse = lax.rsqrt(squares / F + 1e-06) / math.sqrt(F)
    return (widened * inverse[:, None]).astype(jnp.bfloat16)

def reference(features, group_index_list, threshold_codes):
    blocks = ROWS // ROWS_DEV
    normed = lax.map(unit_rows, features.reshape(blocks, ROWS_DEV, F))
    groups = group_index_list.reshape(blocks, ROWS_DEV)
    levels = threshold_codes.reshape(blocks, ROWS_DEV)
    counts = jnp.zeros((blocks, 2, ROWS_DEV), jnp.float32)
    for offset in range(1, MEET + 1):

        def meeting(block_index):
            partner = (block_index + offset) % blocks
            score_matrix = jnp.dot(normed[block_index], normed[partner].T, preferred_element_type=jnp.float32)
            local_portion = count_rows(score_matrix, levels[block_index], groups[block_index], groups[partner])
            mirrored = count_columns(score_matrix, levels[partner], groups[partner], groups[block_index])
            return (local_portion, mirrored)
        local_portion, mirrored = lax.map(meeting, jnp.arange(blocks, dtype=jnp.int32))
        counts = counts + local_portion + jnp.roll(mirrored, offset, axis=0)
    return jnp.transpose(counts, (1, 0, 2)).reshape(2, ROWS)
```

```python
import functools
import math

import jax
import jax.numpy as jnp
from jax import lax
from jax.experimental import pallas as pl
from jax.experimental.pallas import tpu as pltpu
from jax.sharding import PartitionSpec as P

CHUNK = 128
SCALE = math.log2(math.e) / 0.02
MESH = pl.DeviceIdType.MESH
F32 = jnp.float32


def turn(row):
    return jnp.broadcast_to(row, (CHUNK, CHUNK)).T


def kernel(
    rows_count, full_width,
    x_hbm, group_ref, code_ref, out_ref,
    own, slot_a, slot_b, slot_c, unit,
    keep, sent, got,
    squares, squares_in, meta, meta_a, meta_b, meta_c,
    group_own, level_own, group_far, level_far,
    acc_own, acc_far,
    count_a, count_b, count_c, total, in_a, in_b, in_c, in_d, in_f,
    load_sem, fwd_send, a_recv, relay_send, b_recv, back_send, part_send, c_recv,
    job_send, job_recv, small_send, small_recv,
):
    rows, width = own.shape
    half = rows // 2
    steps = rows // CHUNK
    turnover = steps // 2
    me = lax.axis_index("rows")
    feat = lax.axis_index("feat")
    core = lax.rem(me, 2)
    other = me + 1 - 2 * core
    fwd = lax.rem(me + 2, rows_count)
    back = lax.rem(me + rows_count - 2, rows_count)
    fwd_other = lax.rem(other + 2, rows_count)
    back_other = lax.rem(other + rows_count - 2, rows_count)
    mate = (me, 1 - feat)
    first = core == 0
    second = core == 1

    def part(j):
        return pl.ds(pl.multiple_of(j * CHUNK, CHUNK), CHUNK)

    def remote(source, target, send, recv, where):
        return pltpu.make_async_remote_copy(
            src_ref=source, dst_ref=target, send_sem=send, recv_sem=recv,
            device_id=where, device_id_type=MESH,
        )

    def load(j):
        return pltpu.make_async_copy(x_hbm.at[part(j)], own.at[part(j)], load_sem.at[j])

    def fwd_copy(j):
        return remote(x_hbm.at[part(j)], slot_a.at[part(j)], fwd_send.at[j], a_recv.at[j], (fwd, feat))

    def relay_copy(j):
        return remote(slot_a.at[part(j)], slot_b.at[part(j)], relay_send.at[j], b_recv.at[j], (other, feat))

    def back_copy(j):
        return remote(x_hbm.at[part(j)], slot_c.at[part(j)], back_send.at[j], c_recv.at[j], (back, feat))

    def part_copy(j):
        return remote(x_hbm.at[part(j)], slot_c.at[part(j)], part_send.at[j], c_recv.at[j], (other, feat))

    def job_copy(t):
        return remote(sent.at[t], got.at[t], job_send.at[t], job_recv.at[t], mate)

    def small(n, source, target, where):
        return remote(source, target, small_send.at[n], small_recv.at[n], where)

    squares_copy = small(0, squares, squares_in, mate)
    meta_fwd = small(1, meta, meta_a, (fwd, feat))
    meta_fwd_other = small(2, meta, meta_b, (fwd_other, feat))
    meta_back = remote(meta, meta_c, small_send.at[3], small_recv.at[3], (back, feat))
    meta_part = remote(meta, meta_c, small_send.at[4], small_recv.at[3], (other, feat))
    a_home = small(5, count_a, in_a, (back, feat))
    b_home = small(6, count_b, in_b, (back_other, feat))
    c_home_fwd = small(7, count_c, in_c, (fwd, feat))
    c_home_part = small(8, count_c, in_d, (other, feat))
    final = small(9, total, in_f, mate)

    for j in range(steps):
        load(j).start()
    barrier = pltpu.get_barrier_semaphore()
    peers = [(fwd, feat), (fwd_other, feat), (back, feat), (back_other, feat), (other, feat), mate]
    for peer in peers:
        pl.semaphore_signal(barrier, inc=1, device_id=peer, device_id_type=MESH)
    pl.semaphore_wait(barrier, len(peers))

    for j in range(steps):
        fwd_copy(j).start()

    @pl.when(first)
    def _():
        for j in range(steps):
            part_copy(j).start()
        for j in range(steps):
            back_copy(j).start()

    def square(j, carry):
        load(j).wait()
        added = jnp.zeros((CHUNK, CHUNK), F32)
        for t in range(width // CHUNK):
            piece = own[part(j), t * CHUNK : (t + 1) * CHUNK].astype(F32)
            added = added + piece * piece
        squares[0:1, part(j)] = jnp.sum(added.T, axis=0, keepdims=True)
        return carry

    squares[...] = jnp.zeros_like(squares)
    lax.fori_loop(0, steps, square, 0)
    squares_copy.start()
    squares_copy.wait_recv()
    inverse = lax.rsqrt((squares[0:1, :] + squares_in[0:1, :]) / full_width + 1e-06) / math.sqrt(full_width)
    meta[...] = jnp.zeros_like(meta)
    meta[0:1, :] = inverse
    meta[1:2, :] = group_ref[...].astype(F32)
    meta[2:3, :] = jnp.exp2((0.2 + 0.15 * code_ref[...].astype(F32)) * SCALE)
    meta_fwd.start()
    meta_fwd_other.start()

    @pl.when(first)
    def _():
        meta_part.start()
        meta_back.start()

    def normalize(source, j, target, into, meta_ref):
        factor = turn(meta_ref[0:1, part(j)])
        for t in range(width // CHUNK):
            lanes = slice(t * CHUNK, (t + 1) * CHUNK)
            target[into, lanes] = (source[part(j), lanes].astype(F32) * factor).astype(jnp.bfloat16)

    def own_unit(j, carry):
        normalize(own, j, own, part(j), meta)
        return carry

    lax.fori_loop(0, steps, own_unit, 0)

    def columns(meta_ref, group_col, level_col):
        for i in range(half // CHUNK):
            lanes = part(feat * (half // CHUNK) + i)
            group_col[i * CHUNK : (i + 1) * CHUNK, :] = turn(meta_ref[1:2, lanes])
            level_col[i * CHUNK : (i + 1) * CHUNK, :] = turn(meta_ref[2:3, lanes])

    columns(meta, group_own, level_own)
    acc_own[...] = jnp.zeros_like(acc_own)
    acc_far[...] = jnp.zeros_like(acc_far)
    for ref in (count_a, count_b, count_c, total):
        ref[...] = jnp.zeros_like(ref)

    def job(t, fixed, moving, at):
        chunk = moving[at, :]
        for where, target in ((1 - feat, sent), (feat, keep)):
            lines = pl.ds(pl.multiple_of(where * half, half), half)
            target[t] = lax.dot_general(
                fixed[lines, :], chunk, (((1,), (1,)), ((), ())), preferred_element_type=F32
            )
            if target is sent:
                job_copy(t).start()

    size = 32

    def finish(t, j, group_col, level_col, acc, meta_ref, count):
        job_copy(t).wait_recv()
        group_row = jnp.broadcast_to(meta_ref[1:2, part(j)], (size, CHUNK))
        level_row = jnp.broadcast_to(meta_ref[2:3, part(j)], (size, CHUNK))

        def piece(i, carry):
            matched, overall = carry
            at = pl.ds(pl.multiple_of(i * size, size), size)
            power = jnp.exp2((keep[t, at, :] + got[t, at, :]) * (-SCALE))
            mine = 1.0 / (1.0 + level_col[at, :] * power)
            yours = 1.0 / (1.0 + level_row * power)
            same = group_col[at, :] == group_row
            acc[0, at, :] += jnp.where(same, mine, 0.0)
            acc[1, at, :] += mine
            return matched + jnp.where(same, yours, 0.0), overall + yours

        zero = jnp.zeros((size, CHUNK), F32)
        matched, overall = lax.fori_loop(0, half // size, piece, (zero, zero))
        count[0:1, part(j)] += jnp.sum(matched, axis=0, keepdims=True)
        count[1:2, part(j)] += jnp.sum(overall, axis=0, keepdims=True)

    def finish_a(j):
        finish(steps + j, j, group_own, level_own, acc_own, meta_a, count_a)

    def finish_b(j):
        finish(2 * steps + j, j, group_own, level_own, acc_own, meta_b, count_b)

    def finish_near(j):
        finish(j, j, group_own, level_own, acc_own, meta_c, count_c)

    def finish_far(j):
        finish(j, j, group_far, level_far, acc_far, meta_b, count_b)

    meta_wait_c = remote(meta, meta_c, small_send.at[3], small_recv.at[3], (back, feat))

    @pl.when(second)
    def _():
        meta_wait_c.wait_recv()

        def step(j, carry):
            part_copy(j).wait_recv()
            normalize(slot_c, j, slot_c, part(j), meta_c)
            job(j, own, slot_c, part(j))
            return carry

        lax.fori_loop(0, steps, step, 0)

    meta_fwd.wait_recv()
    meta_fwd_other.wait_recv()

    def main(j, carry):
        @pl.when(j > 0)
        def _():
            finish_a(j - 1)
            finish_b(j - 1)

        @pl.when(second)
        def _():
            finish_near(j)

        @pl.when(jnp.logical_and(first, j > turnover))
        def _():
            def old(i, carry):
                finish_far(i)
                return carry

            lax.fori_loop(jnp.where(j == turnover + 1, 0, j - 1), j, old, 0)

        fwd_copy(j).wait_recv()
        relay_copy(j).start()
        normalize(slot_a, j, unit, slice(0, CHUNK), meta_a)
        job(steps + j, own, unit, slice(0, CHUNK))
        relay_copy(j).wait_recv()
        normalize(slot_b, j, slot_b, part(j), meta_b)
        job(2 * steps + j, own, slot_b, part(j))

        @pl.when(jnp.logical_and(first, j == turnover))
        def _():
            meta_wait_c.wait_recv()

            def ready(i, carry):
                back_copy(i).wait_recv()
                normalize(slot_c, i, slot_c, part(i), meta_c)
                return carry

            lax.fori_loop(0, steps, ready, 0)
            columns(meta_c, group_far, level_far)

        @pl.when(jnp.logical_and(first, j >= turnover))
        def _():
            def far(i, carry):
                job(i, slot_c, slot_b, part(i))
                return carry

            lax.fori_loop(jnp.where(j == turnover, 0, j), j + 1, far, 0)

        return carry

    lax.fori_loop(0, steps, main, 0)
    finish_a(steps - 1)
    a_home.start()
    finish_b(steps - 1)

    def fold(acc, count, add):
        for i in range(half // CHUNK):
            lanes = part(feat * (half // CHUNK) + i)
            for n in range(2):
                value = jnp.sum(acc[n, i * CHUNK : (i + 1) * CHUNK, :].T, axis=0, keepdims=True)
                count[n : n + 1, lanes] = value

    @pl.when(first)
    def _():
        finish_far(steps - 1)
        fold(acc_far, count_c, False)

    b_home.start()

    @pl.when(first)
    def _():
        c_home_fwd.start()

    @pl.when(second)
    def _():
        c_home_part.start()

    fold(acc_own, total, False)
    a_home.wait_recv()
    b_home.wait_recv()
    total[...] += in_a[...] + in_b[...]

    @pl.when(first)
    def _():
        c_home_fwd.wait_recv()
        c_home_part.wait_recv()
        total[...] += in_c[...] + in_d[...]

    final.start()
    final.wait_recv()
    matched = total[0:1, :] + in_f[0:1, :]
    overall = total[1:2, :] + in_f[1:2, :]
    out_ref[0:1, :] = matched
    out_ref[1:2, :] = overall - matched

    def drain(j, carry):
        fwd_copy(j).wait_send()
        relay_copy(j).wait_send()
        return carry

    lax.fori_loop(0, steps, drain, 0)

    def drain_jobs(t, carry):
        job_copy(t).wait_send()
        return carry

    lax.fori_loop(0, 3 * steps, drain_jobs, 0)
    for copy in (squares_copy, meta_fwd, meta_fwd_other, a_home, b_home, final):
        copy.wait_send()

    @pl.when(first)
    def _():
        def drain_c(j, carry):
            part_copy(j).wait_send()
            back_copy(j).wait_send()
            return carry

        lax.fori_loop(0, steps, drain_c, 0)
        meta_part.wait_send()
        meta_back.wait_send()
        c_home_fwd.wait_send()

    @pl.when(second)
    def _():
        c_home_part.wait_send()


def local(rows_count, features, group_index_list, threshold_codes):
    rows, width = features.shape
    full_width = width * lax.axis_size("feat")
    half = rows // 2
    steps = rows // CHUNK
    block = pltpu.VMEM((rows, width), jnp.bfloat16)
    tiles = pltpu.VMEM((3 * steps, half, CHUNK), F32)
    line = pltpu.VMEM((8, rows), F32)
    column = pltpu.VMEM((half, CHUNK), F32)
    sums = pltpu.VMEM((2, half, CHUNK), F32)
    sems = pltpu.SemaphoreType.DMA((steps,))
    vmem = pl.BlockSpec(memory_space=pltpu.VMEM)
    return pl.pallas_call(
        functools.partial(kernel, rows_count, full_width),
        out_shape=jax.ShapeDtypeStruct((2, rows), F32),
        in_specs=[pl.BlockSpec(memory_space=pl.ANY), vmem, vmem],
        out_specs=vmem,
        scratch_shapes=[
            block, block, block, block, pltpu.VMEM((CHUNK, width), jnp.bfloat16),
            tiles, tiles, tiles,
            *[line] * 6,
            *[column] * 4,
            sums, sums,
            *[line] * 9,
            *[sems] * 8,
            pltpu.SemaphoreType.DMA((3 * steps,)), pltpu.SemaphoreType.DMA((3 * steps,)),
            pltpu.SemaphoreType.DMA((10,)), pltpu.SemaphoreType.DMA((10,)),
        ],
        compiler_params=pltpu.CompilerParams(
            collective_id=0, has_side_effects=True, vmem_limit_bytes=56 * 1024 * 1024
        ),
    )(features, group_index_list.reshape(1, rows), threshold_codes.reshape(1, rows))


def solution(mesh):
    placed = (P("rows", "feat"), P("rows"), P("rows"))
    return jax.shard_map(
        functools.partial(local, mesh.shape["rows"]),
        mesh=mesh, in_specs=placed, out_specs=P(None, "rows"), check_vma=False,
    )
```

```python
import functools
import math

import jax
import jax.numpy as jnp
from jax import lax
from jax.experimental import pallas as pl
from jax.experimental.pallas import tpu as pltpu
from jax.sharding import PartitionSpec as P

CHUNK = 128
SCALE = math.log2(math.e) / 0.02
MESH = pl.DeviceIdType.MESH
PLANE = 16
GRID = 32000.0
F32 = jnp.float32


def turn(row):
    return jnp.broadcast_to(row, (CHUNK, CHUNK)).T


def kernel(
    rows_count, full_width,
    x_hbm, group_ref, code_ref, out_ref,
    own, slot_a, slot_b, slot_c, hop, unit,
    keep, sent, got,
    squares, squares_in, meta, meta_a, meta_b, meta_c,
    group_own, level_own, group_far, level_far,
    acc_own, acc_far,
    count_a, count_b, count_c, total, in_a, in_b, in_c, in_d, in_f,
    load_sem, fwd_send, a_recv, relay_send, b_recv, back_send, part_send, c_recv,
    job_send, job_recv, small_send, small_recv, hop_send, hop_recv,
):
    rows, width = own.shape
    half = rows // 2
    steps = rows // CHUNK
    turnover = steps - 2
    me = lax.axis_index("rows")
    feat = lax.axis_index("feat")
    core = lax.rem(me, 2)
    other = me + 1 - 2 * core
    fwd = lax.rem(me + 2, rows_count)
    back = lax.rem(me + rows_count - 2, rows_count)
    fwd_other = lax.rem(other + 2, rows_count)
    back_other = lax.rem(other + rows_count - 2, rows_count)
    mate = (me, 1 - feat)
    first = core == 0
    second = core == 1
    place = lax.rem(me // 2, PLANE)
    low, next_low, side, next_high, high = (place == n for n in (0, 1, PLANE - 4, PLANE - 2, PLANE - 1))
    bound = 2 * PLANE

    def shift(n):
        return (lax.rem(me + n + rows_count, rows_count), feat)

    def part(j):
        return pl.ds(pl.multiple_of(j * CHUNK, CHUNK), CHUNK)

    def remote(source, target, send, recv, where):
        return pltpu.make_async_remote_copy(
            src_ref=source, dst_ref=target, send_sem=send, recv_sem=recv,
            device_id=where, device_id_type=MESH,
        )

    by_side = {1: 0, 4: 1}
    by_row = {2: 0, 5: 1}
    straight = (0, 3)

    def leg_copy(j):
        slot = by_side[j] if j in by_side else by_row[j]
        return remote(
            x_hbm.at[part(j)], hop.at[slot], fwd_send.at[j], hop_recv.at[slot], shift(-6 if j in by_side else -2)
        )

    def side_copy(j):
        return remote(hop.at[by_side[j]], slot_a.at[part(j)], hop_send.at[by_side[j]], a_recv.at[j], shift(8))

    def row_copy(j):
        slot = by_row[j]
        return remote(hop.at[slot], hop.at[slot], hop_send.at[slot], hop_recv.at[slot], shift(6))

    def last_copy(j):
        return remote(hop.at[by_row[j]], slot_a.at[part(j)], hop_send.at[by_row[j]], a_recv.at[j], shift(-2))

    def back_leg_copy(j):
        return remote(x_hbm.at[part(j)], hop.at[j], back_send.at[j], hop_recv.at[j], shift(bound - 2))

    def high_copy(j):
        return remote(hop.at[j], slot_c.at[part(j)], hop_send.at[j], c_recv.at[j], shift(-bound))

    def send_fwd(js):
        @pl.when(jnp.logical_not(high))
        def _():
            for j in js:
                fwd_copy(j).start()

    def send_back(js):
        @pl.when(jnp.logical_and(first, low))
        def _():
            for j in js:
                (back_leg_copy(j) if j < steps // 2 else back_copy(j)).start()

        @pl.when(jnp.logical_and(first, jnp.logical_not(low)))
        def _():
            for j in js:
                back_copy(j).start()

    def pass_on(*legs):
        for arrived, copy in legs:
            arrived.wait_recv()
            copy.start()

    def load(j):
        return pltpu.make_async_copy(x_hbm.at[part(j)], own.at[part(j)], load_sem.at[j])

    def fwd_copy(j):
        return remote(x_hbm.at[part(j)], slot_a.at[part(j)], fwd_send.at[j], a_recv.at[j], (fwd, feat))

    def relay_copy(j):
        return remote(slot_a.at[part(j)], slot_b.at[part(j)], relay_send.at[j], b_recv.at[j], (other, feat))

    def back_copy(j):
        return remote(x_hbm.at[part(j)], slot_c.at[part(j)], back_send.at[j], c_recv.at[j], (back, feat))

    def part_copy(j):
        return remote(x_hbm.at[part(j)], slot_c.at[part(j)], part_send.at[j], c_recv.at[j], (other, feat))

    def job_copy(t):
        return remote(sent.at[t], got.at[t], job_send.at[t], job_recv.at[t], mate)

    def small(n, source, target, where):
        return remote(source, target, small_send.at[n], small_recv.at[n], where)

    squares_copy = small(0, squares, squares_in, mate)
    meta_fwd = small(1, meta, meta_a, (fwd, feat))
    meta_fwd_other = small(2, meta, meta_b, (fwd_other, feat))
    meta_back = remote(meta, meta_c, small_send.at[3], small_recv.at[3], (back, feat))
    meta_part = remote(meta, meta_c, small_send.at[4], small_recv.at[3], (other, feat))
    a_home = small(5, count_a, in_a, (back, feat))
    b_home = small(6, count_b, in_b, (back_other, feat))
    c_home_fwd = small(7, count_c, in_c, (fwd, feat))
    c_home_part = small(8, count_c, in_d, (other, feat))
    final = small(9, total, in_f, mate)

    for j in range(steps):
        load(j).start()
    barrier = pltpu.get_barrier_semaphore()
    peers = [(fwd, feat), (fwd_other, feat), (back, feat), (back_other, feat), (other, feat), mate]
    for peer in peers:
        pl.semaphore_signal(barrier, inc=1, device_id=peer, device_id_type=MESH)
    expected = len(peers)
    for role, offsets in (
        (low, (bound - 2, -8)), (side, (6, 8)), (high, (2 - bound, -6, bound, -bound)),
        (next_high, (6,)), (next_low, (-6,)),
    ):
        @pl.when(role)
        def _():
            for offset in offsets:
                pl.semaphore_signal(barrier, inc=1, device_id=shift(offset), device_id_type=MESH)

        expected += len(offsets) * role.astype(jnp.int32)
    pl.semaphore_wait(barrier, expected)

    @pl.when(high)
    def _():
        for j in by_row:
            leg_copy(j).start()
        fwd_copy(straight[0]).start()
        leg_copy(1).start()

    send_fwd((0,))
    send_back((0,))

    @pl.when(first)
    def _():
        for j in range(steps):
            part_copy(j).start()

    def square(j, carry):
        load(j).wait()
        added = jnp.zeros((CHUNK, CHUNK), F32)
        for t in range(width // CHUNK):
            piece = own[part(j), t * CHUNK : (t + 1) * CHUNK].astype(F32)
            added = added + piece * piece
        squares[0:1, part(j)] = jnp.sum(added.T, axis=0, keepdims=True)
        return carry

    squares[...] = jnp.zeros_like(squares)
    lax.fori_loop(0, steps, square, 0)
    squares_copy.start()
    squares_copy.wait_recv()
    inverse = lax.rsqrt((squares[0:1, :] + squares_in[0:1, :]) / full_width + 1e-06) / math.sqrt(full_width)
    meta[...] = jnp.zeros_like(meta)
    meta[0:1, :] = inverse
    meta[1:2, :] = group_ref[...].astype(F32)
    meta[2:3, :] = jnp.exp2((0.2 + 0.15 * code_ref[...].astype(F32)) * SCALE)
    meta_fwd.start()
    meta_fwd_other.start()

    @pl.when(first)
    def _():
        meta_part.start()
        meta_back.start()

    @pl.when(high)
    def _():
        leg_copy(4).start()

    send_fwd((1, 2, 3, 4, 5))
    send_back((1, 2, 3, 4, 5))

    def normalize(source, j, target, into, meta_ref):
        factor = turn(meta_ref[0:1, part(j)])
        for t in range(width // CHUNK):
            lanes = slice(t * CHUNK, (t + 1) * CHUNK)
            target[into, lanes] = (source[part(j), lanes].astype(F32) * factor).astype(jnp.bfloat16)

    def own_unit(j, carry):
        normalize(own, j, own, part(j), meta)
        return carry

    lax.fori_loop(0, steps, own_unit, 0)

    def columns(meta_ref, group_col, level_col):
        for i in range(half // CHUNK):
            lanes = part(feat * (half // CHUNK) + i)
            group_col[i * CHUNK : (i + 1) * CHUNK, :] = turn(meta_ref[1:2, lanes])
            level_col[i * CHUNK : (i + 1) * CHUNK, :] = turn(meta_ref[2:3, lanes])

    columns(meta, group_own, level_own)
    acc_own[...] = jnp.zeros_like(acc_own)
    acc_far[...] = jnp.zeros_like(acc_far)
    for ref in (count_a, count_b, count_c, total):
        ref[...] = jnp.zeros_like(ref)

    def job(t, fixed, moving, at):
        chunk = moving[at, :]
        for where, target in ((1 - feat, sent), (feat, keep)):
            lines = pl.ds(pl.multiple_of(where * half, half), half)
            value = lax.dot_general(
                fixed[lines, :], chunk, (((1,), (1,)), ((), ())), preferred_element_type=F32
            )
            if target is sent:
                value = jnp.round(value * GRID).astype(jnp.int32).astype(jnp.int16)
            target[t] = value
            if target is sent:
                job_copy(t).start()

    size = 32

    def finish(t, j, group_col, level_col, acc, meta_ref, count):
        job_copy(t).wait_recv()
        group_row = jnp.broadcast_to(meta_ref[1:2, part(j)], (size, CHUNK))
        level_row = jnp.broadcast_to(meta_ref[2:3, part(j)], (size, CHUNK))

        def piece(i, carry):
            matched, overall = carry
            at = pl.ds(pl.multiple_of(i * size, size), size)
            power = jnp.exp2(keep[t, at, :] * (-SCALE) + got[t, at, :].astype(F32) * (-SCALE / GRID))
            mine = 1.0 / (1.0 + level_col[at, :] * power)
            yours = 1.0 / (1.0 + level_row * power)
            same = group_col[at, :] == group_row
            acc[0, at, :] += jnp.where(same, mine, 0.0)
            acc[1, at, :] += mine
            return matched + jnp.where(same, yours, 0.0), overall + yours

        zero = jnp.zeros((size, CHUNK), F32)
        matched, overall = lax.fori_loop(0, half // size, piece, (zero, zero))
        count[0:1, part(j)] += jnp.sum(matched, axis=0, keepdims=True)
        count[1:2, part(j)] += jnp.sum(overall, axis=0, keepdims=True)

    def finish_a(j):
        finish(steps + j, j, group_own, level_own, acc_own, meta_a, count_a)

    def finish_b(j):
        finish(2 * steps + j, j, group_own, level_own, acc_own, meta_b, count_b)

    def finish_near(j):
        finish(j, j, group_own, level_own, acc_own, meta_c, count_c)

    def finish_far(j):
        finish(j, j, group_far, level_far, acc_far, meta_b, count_b)

    meta_wait_c = remote(meta, meta_c, small_send.at[3], small_recv.at[3], (back, feat))

    @pl.when(second)
    def _():
        meta_wait_c.wait_recv()

        def step(j, carry):
            part_copy(j).wait_recv()
            normalize(slot_c, j, slot_c, part(j), meta_c)
            job(j, own, slot_c, part(j))
            return carry

        lax.fori_loop(0, steps, step, 0)

    meta_fwd.wait_recv()
    meta_fwd_other.wait_recv()

    def main(j, carry):
        for turn_at, role, act in (
            (1, high, lambda: fwd_copy(straight[1]).start()),
            (1, side, lambda: pass_on((leg_copy(1), side_copy(1)))),
            (3, side, lambda: pass_on((leg_copy(4), side_copy(4)))),
            (1, next_high, lambda: pass_on((leg_copy(2), row_copy(2)))),
            (3, next_high, lambda: pass_on((leg_copy(5), row_copy(5)))),
            (3, next_low, lambda: pass_on((row_copy(2), last_copy(2)))),
            (5, next_low, lambda: pass_on((row_copy(5), last_copy(5)))),
            (1, jnp.logical_and(first, high), lambda: pass_on(*((back_leg_copy(i), high_copy(i)) for i in (0, 1)))),
            (2, jnp.logical_and(first, high), lambda: pass_on((back_leg_copy(2), high_copy(2)))),
        ):
            pl.when(jnp.logical_and(j == turn_at, role))(act)

        @pl.when(j > 1)
        def _():
            finish_a(j - 2)
            finish_b(j - 2)

        @pl.when(second)
        def _():
            finish_near(j)

        @pl.when(jnp.logical_and(first, j > turnover))
        def _():
            def old(i, carry):
                finish_far(i)
                return carry

            lax.fori_loop(jnp.where(j == turnover + 1, 0, j - 1), j, old, 0)

        fwd_copy(j).wait_recv()
        relay_copy(j).start()
        normalize(slot_a, j, unit, slice(0, CHUNK), meta_a)
        job(steps + j, own, unit, slice(0, CHUNK))
        relay_copy(j).wait_recv()
        normalize(slot_b, j, slot_b, part(j), meta_b)
        job(2 * steps + j, own, slot_b, part(j))

        @pl.when(jnp.logical_and(first, j == turnover))
        def _():
            meta_wait_c.wait_recv()

            def ready(i, carry):
                back_copy(i).wait_recv()
                normalize(slot_c, i, slot_c, part(i), meta_c)
                return carry

            lax.fori_loop(0, steps, ready, 0)
            columns(meta_c, group_far, level_far)

        @pl.when(jnp.logical_and(first, j >= turnover))
        def _():
            def far(i, carry):
                job(i, slot_c, slot_b, part(i))
                return carry

            lax.fori_loop(jnp.where(j == turnover, 0, j), j + 1, far, 0)

        return carry

    lax.fori_loop(0, steps, main, 0)
    finish_a(steps - 2)
    finish_b(steps - 2)
    finish_a(steps - 1)
    a_home.start()
    finish_b(steps - 1)

    def fold(acc, count, add):
        for i in range(half // CHUNK):
            lanes = part(feat * (half // CHUNK) + i)
            for n in range(2):
                value = jnp.sum(acc[n, i * CHUNK : (i + 1) * CHUNK, :].T, axis=0, keepdims=True)
                count[n : n + 1, lanes] = value

    @pl.when(first)
    def _():
        finish_far(steps - 1)
        fold(acc_far, count_c, False)

    b_home.start()

    @pl.when(first)
    def _():
        c_home_fwd.start()

    @pl.when(second)
    def _():
        c_home_part.start()

    fold(acc_own, total, False)
    a_home.wait_recv()
    b_home.wait_recv()
    total[...] += in_a[...] + in_b[...]

    @pl.when(first)
    def _():
        c_home_fwd.wait_recv()
        c_home_part.wait_recv()
        total[...] += in_c[...] + in_d[...]

    final.start()
    final.wait_recv()
    matched = total[0:1, :] + in_f[0:1, :]
    overall = total[1:2, :] + in_f[1:2, :]
    out_ref[0:1, :] = matched
    out_ref[1:2, :] = overall - matched

    def drain(j, carry):
        fwd_copy(j).wait_send()
        relay_copy(j).wait_send()
        return carry

    lax.fori_loop(0, steps, drain, 0)
    for role, copies in (
        (side, (side_copy(1), side_copy(4))), (next_high, (row_copy(2), row_copy(5))),
        (next_low, (last_copy(2), last_copy(5))),
        (jnp.logical_and(first, high), (high_copy(0), high_copy(1), high_copy(2))),
    ):
        @pl.when(role)
        def _():
            for copy in copies:
                copy.wait_send()


    def drain_jobs(t, carry):
        job_copy(t).wait_send()
        return carry

    lax.fori_loop(0, 3 * steps, drain_jobs, 0)
    for copy in (squares_copy, meta_fwd, meta_fwd_other, a_home, b_home, final):
        copy.wait_send()

    @pl.when(first)
    def _():
        def drain_c(j, carry):
            part_copy(j).wait_send()
            back_copy(j).wait_send()
            return carry

        lax.fori_loop(0, steps, drain_c, 0)
        meta_part.wait_send()
        meta_back.wait_send()
        c_home_fwd.wait_send()

    @pl.when(second)
    def _():
        c_home_part.wait_send()


def local(rows_count, features, group_index_list, threshold_codes):
    rows, width = features.shape
    full_width = width * lax.axis_size("feat")
    half = rows // 2
    steps = rows // CHUNK
    block = pltpu.VMEM((rows, width), jnp.bfloat16)
    tiles = pltpu.VMEM((3 * steps, half, CHUNK), F32)
    coded = pltpu.VMEM((3 * steps, half, CHUNK), jnp.int16)
    hops = steps // 2
    line = pltpu.VMEM((8, rows), F32)
    column = pltpu.VMEM((half, CHUNK), F32)
    sums = pltpu.VMEM((2, half, CHUNK), F32)
    sems = pltpu.SemaphoreType.DMA((steps,))
    vmem = pl.BlockSpec(memory_space=pltpu.VMEM)
    return pl.pallas_call(
        functools.partial(kernel, rows_count, full_width),
        out_shape=jax.ShapeDtypeStruct((2, rows), F32),
        in_specs=[pl.BlockSpec(memory_space=pl.ANY), vmem, vmem],
        out_specs=vmem,
        scratch_shapes=[
            block, block, block, block, pltpu.VMEM((hops, CHUNK, width), jnp.bfloat16),
            pltpu.VMEM((CHUNK, width), jnp.bfloat16),
            tiles, coded, coded,
            *[line] * 6,
            *[column] * 4,
            sums, sums,
            *[line] * 9,
            *[sems] * 8,
            pltpu.SemaphoreType.DMA((3 * steps,)), pltpu.SemaphoreType.DMA((3 * steps,)),
            pltpu.SemaphoreType.DMA((10,)), pltpu.SemaphoreType.DMA((10,)),
            pltpu.SemaphoreType.DMA((hops,)), pltpu.SemaphoreType.DMA((hops,)),
        ],
        compiler_params=pltpu.CompilerParams(
            collective_id=0, has_side_effects=True, vmem_limit_bytes=56 * 1024 * 1024
        ),
    )(features, group_index_list.reshape(1, rows), threshold_codes.reshape(1, rows))


def solution(mesh):
    placed = (P("rows", "feat"), P("rows"), P("rows"))
    return jax.shard_map(
        functools.partial(local, mesh.shape["rows"]),
        mesh=mesh, in_specs=placed, out_specs=P(None, "rows"), check_vma=False,
    )
```

```python
import functools
import math

import jax
import jax.numpy as jnp
from jax import lax
from jax.experimental import pallas as pl
from jax.experimental.pallas import tpu as pltpu
from jax.sharding import PartitionSpec as P

CHUNK = 128
SCALE = math.log2(math.e) / 0.02
MESH = pl.DeviceIdType.MESH
PLANE = 16
GRID = 32000.0
F32 = jnp.float32


def turn(row):
    return jnp.broadcast_to(row, (CHUNK, CHUNK)).T


def kernel(
    rows_count, full_width,
    x_hbm, group_ref, code_ref, out_ref,
    own, slot_a, slot_b, slot_c, hop, unit,
    keep, sent, got, keep_pair, sent_pair, got_pair,
    squares, squares_in, meta, meta_a, meta_b, meta_c,
    group_own, level_own, group_far, level_far,
    acc_own, acc_far,
    count_a, count_b, count_c, total, in_a, in_b, in_c, in_d, in_f,
    load_sem, fwd_send, a_recv, relay_send, b_recv, back_send, part_send, c_recv,
    job_send, job_recv, pair_send, pair_recv, small_send, small_recv, hop_send, hop_recv,
):
    rows, width = own.shape
    half = rows // 2
    steps = rows // CHUNK
    turnover = steps - 2
    me = lax.axis_index("rows")
    feat = lax.axis_index("feat")
    core = lax.rem(me, 2)
    other = me + 1 - 2 * core
    fwd = lax.rem(me + 2, rows_count)
    back = lax.rem(me + rows_count - 2, rows_count)
    fwd_other = lax.rem(other + 2, rows_count)
    back_other = lax.rem(other + rows_count - 2, rows_count)
    mate = (me, 1 - feat)
    first = core == 0
    second = core == 1
    place = lax.rem(me // 2, PLANE)
    low, next_low, side, next_high, high = (place == n for n in (0, 1, PLANE - 4, PLANE - 2, PLANE - 1))
    bound = 2 * PLANE

    def shift(n):
        return (lax.rem(me + n + rows_count, rows_count), feat)

    def part(j):
        return pl.ds(pl.multiple_of(j * CHUNK, CHUNK), CHUNK)

    def remote(source, target, send, recv, where):
        return pltpu.make_async_remote_copy(
            src_ref=source, dst_ref=target, send_sem=send, recv_sem=recv,
            device_id=where, device_id_type=MESH,
        )

    by_side = {1: 0, 4: 1}
    by_row = {2: 0, 5: 1}
    straight = (0, 3)

    def leg_copy(j):
        slot = by_side[j] if j in by_side else by_row[j]
        return remote(
            x_hbm.at[part(j)], hop.at[slot], fwd_send.at[j], hop_recv.at[slot], shift(-6 if j in by_side else -2)
        )

    def side_copy(j):
        return remote(hop.at[by_side[j]], slot_a.at[part(j)], hop_send.at[by_side[j]], a_recv.at[j], shift(8))

    def row_copy(j):
        slot = by_row[j]
        return remote(hop.at[slot], hop.at[slot], hop_send.at[slot], hop_recv.at[slot], shift(6))

    def last_copy(j):
        return remote(hop.at[by_row[j]], slot_a.at[part(j)], hop_send.at[by_row[j]], a_recv.at[j], shift(-2))

    def back_leg_copy(j):
        return remote(x_hbm.at[part(j)], hop.at[j], back_send.at[j], hop_recv.at[j], shift(bound - 2))

    def high_copy(j):
        return remote(hop.at[j], slot_c.at[part(j)], hop_send.at[j], c_recv.at[j], shift(-bound))

    def send_fwd(js):
        @pl.when(jnp.logical_not(high))
        def _():
            for j in js:
                fwd_copy(j).start()

    def send_back(js):
        @pl.when(jnp.logical_and(first, low))
        def _():
            for j in js:
                (back_leg_copy(j) if j < steps // 2 else back_copy(j)).start()

        @pl.when(jnp.logical_and(first, jnp.logical_not(low)))
        def _():
            for j in js:
                back_copy(j).start()

    def pass_on(*legs):
        for arrived, copy in legs:
            arrived.wait_recv()
            copy.start()

    def load(j):
        return pltpu.make_async_copy(x_hbm.at[part(j)], own.at[part(j)], load_sem.at[j])

    def fwd_copy(j):
        return remote(x_hbm.at[part(j)], slot_a.at[part(j)], fwd_send.at[j], a_recv.at[j], (fwd, feat))

    def relay_copy(j):
        return remote(slot_a.at[part(j)], slot_b.at[part(j)], relay_send.at[j], b_recv.at[j], (other, feat))

    def back_copy(j):
        return remote(x_hbm.at[part(j)], slot_c.at[part(j)], back_send.at[j], c_recv.at[j], (back, feat))

    def part_copy(j):
        return remote(x_hbm.at[part(j)], slot_c.at[part(j)], part_send.at[j], c_recv.at[j], (other, feat))

    def job_copy(t):
        return remote(sent.at[t], got.at[t], job_send.at[t], job_recv.at[t], mate)

    def pair_copy(t):
        return remote(sent_pair.at[t], got_pair.at[t], pair_send.at[t], pair_recv.at[t], mate)

    def small(n, source, target, where):
        return remote(source, target, small_send.at[n], small_recv.at[n], where)

    squares_copy = small(0, squares, squares_in, mate)
    meta_fwd = small(1, meta, meta_a, (fwd, feat))
    meta_fwd_other = small(2, meta, meta_b, (fwd_other, feat))
    meta_back = remote(meta, meta_c, small_send.at[3], small_recv.at[3], (back, feat))
    meta_part = remote(meta, meta_c, small_send.at[4], small_recv.at[3], (other, feat))
    a_home = small(5, count_a, in_a, (back, feat))
    b_home = small(6, count_b, in_b, (back_other, feat))
    c_home_fwd = small(7, count_c, in_c, (fwd, feat))
    c_home_part = small(8, count_c, in_d, (other, feat))
    final = small(9, total, in_f, mate)

    for j in range(steps):
        load(j).start()
    barrier = pltpu.get_barrier_semaphore()
    peers = [(fwd, feat), (fwd_other, feat), (back, feat), (back_other, feat), (other, feat), mate]
    for peer in peers:
        pl.semaphore_signal(barrier, inc=1, device_id=peer, device_id_type=MESH)
    expected = len(peers)
    for role, offsets in (
        (low, (bound - 2, -8)), (side, (6, 8)), (high, (2 - bound, -6, bound, -bound)),
        (next_high, (6,)), (next_low, (-6,)),
    ):
        @pl.when(role)
        def _():
            for offset in offsets:
                pl.semaphore_signal(barrier, inc=1, device_id=shift(offset), device_id_type=MESH)

        expected += len(offsets) * role.astype(jnp.int32)
    pl.semaphore_wait(barrier, expected)

    @pl.when(high)
    def _():
        for j in by_row:
            leg_copy(j).start()
        leg_copy(1).start()

    send_fwd((0,))
    send_back((0,))

    @pl.when(first)
    def _():
        for j in range(steps):
            part_copy(j).start()

    def square(j, carry):
        load(j).wait()
        added = jnp.zeros((CHUNK, CHUNK), F32)
        for t in range(width // CHUNK):
            piece = own[part(j), t * CHUNK : (t + 1) * CHUNK].astype(F32)
            added = added + piece * piece
        squares[0:1, part(j)] = jnp.sum(added.T, axis=0, keepdims=True)
        return carry

    squares[...] = jnp.zeros_like(squares)
    lax.fori_loop(0, steps, square, 0)
    squares_copy.start()
    squares_copy.wait_recv()
    inverse = lax.rsqrt((squares[0:1, :] + squares_in[0:1, :]) / full_width + 1e-06) / math.sqrt(full_width)
    meta[...] = jnp.zeros_like(meta)
    meta[0:1, :] = inverse
    meta[1:2, :] = group_ref[...].astype(F32)
    meta[2:3, :] = jnp.exp2((0.2 + 0.15 * code_ref[...].astype(F32)) * SCALE)
    meta_fwd.start()
    meta_fwd_other.start()

    @pl.when(first)
    def _():
        meta_part.start()
        meta_back.start()

    @pl.when(high)
    def _():
        leg_copy(4).start()
        fwd_copy(straight[0]).start()

    send_fwd((1, 2, 3, 4, 5))
    send_back((1, 2, 3, 4, 5))

    def normalize(source, j, target, into, meta_ref, also=None):
        factor = turn(meta_ref[0:1, part(j)])
        for t in range(width // CHUNK):
            lanes = slice(t * CHUNK, (t + 1) * CHUNK)
            value = (source[part(j), lanes].astype(F32) * factor).astype(jnp.bfloat16)
            target[into, lanes] = value
            if also is not None:
                also[CHUNK:, lanes] = value

    def own_unit(j, carry):
        normalize(own, j, own, part(j), meta)
        return carry

    lax.fori_loop(0, steps, own_unit, 0)

    def columns(meta_ref, group_col, level_col):
        for i in range(half // CHUNK):
            lanes = part(feat * (half // CHUNK) + i)
            group_col[i * CHUNK : (i + 1) * CHUNK, :] = turn(meta_ref[1:2, lanes])
            level_col[i * CHUNK : (i + 1) * CHUNK, :] = turn(meta_ref[2:3, lanes])

    columns(meta, group_own, level_own)
    acc_own[...] = jnp.zeros_like(acc_own)
    acc_far[...] = jnp.zeros_like(acc_far)
    for ref in (count_a, count_b, count_c, total):
        ref[...] = jnp.zeros_like(ref)

    def job(fixed, chunk, t, held, outgoing, copy):
        for where, target in ((1 - feat, outgoing), (feat, held)):
            lines = pl.ds(pl.multiple_of(where * half, half), half)
            value = lax.dot_general(
                fixed[lines, :], chunk, (((1,), (1,)), ((), ())), preferred_element_type=F32
            )
            if target is outgoing:
                target[t] = jnp.round(value * GRID).astype(jnp.int32).astype(jnp.int16)
                copy(t).start()
            else:
                target[t] = value

    def single(t, fixed, moving, at):
        job(fixed, moving[at, :], t, keep, sent, job_copy)

    size = 32

    def finish(held, arrived, t, lanes, j, group_col, level_col, acc, meta_ref, count):
        group_row = jnp.broadcast_to(meta_ref[1:2, part(j)], (size, CHUNK))
        level_row = jnp.broadcast_to(meta_ref[2:3, part(j)], (size, CHUNK))

        def piece(i, carry):
            matched, overall = carry
            at = pl.ds(pl.multiple_of(i * size, size), size)
            power = jnp.exp2(held[t, at, lanes] * (-SCALE) + arrived[t, at, lanes].astype(F32) * (-SCALE / GRID))
            mine = 1.0 / (1.0 + level_col[at, :] * power)
            yours = 1.0 / (1.0 + level_row * power)
            same = group_col[at, :] == group_row
            acc[0, at, :] += jnp.where(same, mine, 0.0)
            acc[1, at, :] += mine
            return matched + jnp.where(same, yours, 0.0), overall + yours

        zero = jnp.zeros((size, CHUNK), F32)
        matched, overall = lax.fori_loop(0, half // size, piece, (zero, zero))
        count[0:1, part(j)] += jnp.sum(matched, axis=0, keepdims=True)
        count[1:2, part(j)] += jnp.sum(overall, axis=0, keepdims=True)

    every, left, right = slice(0, CHUNK), slice(0, CHUNK), slice(CHUNK, 2 * CHUNK)

    def finish_a(j):
        pair_copy(j).wait_recv()
        finish(keep_pair, got_pair, j, left, j, group_own, level_own, acc_own, meta_a, count_a)

    def finish_b(j):
        finish(keep_pair, got_pair, j, right, j, group_own, level_own, acc_own, meta_b, count_b)

    def finish_near(j):
        job_copy(j).wait_recv()
        finish(keep, got, j, every, j, group_own, level_own, acc_own, meta_c, count_c)

    def finish_far(j):
        job_copy(j).wait_recv()
        finish(keep, got, j, every, j, group_far, level_far, acc_far, meta_b, count_b)

    meta_wait_c = remote(meta, meta_c, small_send.at[3], small_recv.at[3], (back, feat))

    @pl.when(second)
    def _():
        meta_wait_c.wait_recv()

        def step(j, carry):
            part_copy(j).wait_recv()
            normalize(slot_c, j, slot_c, part(j), meta_c)
            single(j, own, slot_c, part(j))
            return carry

        lax.fori_loop(0, steps, step, 0)

    meta_fwd.wait_recv()
    meta_fwd_other.wait_recv()

    def main(j, carry):
        for turn_at, role, act in (
            (1, high, lambda: fwd_copy(straight[1]).start()),
            (0, side, lambda: pass_on((leg_copy(1), side_copy(1)))),
            (2, side, lambda: pass_on((leg_copy(4), side_copy(4)))),
            (0, next_high, lambda: pass_on((leg_copy(2), row_copy(2)))),
            (2, next_high, lambda: pass_on((leg_copy(5), row_copy(5)))),
            (3, next_low, lambda: pass_on((row_copy(2), last_copy(2)))),
            (5, next_low, lambda: pass_on((row_copy(5), last_copy(5)))),
            (1, jnp.logical_and(first, high), lambda: pass_on(*((back_leg_copy(i), high_copy(i)) for i in (0, 1)))),
            (2, jnp.logical_and(first, high), lambda: pass_on((back_leg_copy(2), high_copy(2)))),
        ):
            pl.when(jnp.logical_and(j == turn_at, role))(act)

        @pl.when(j > 1)
        def _():
            finish_a(j - 2)
            finish_b(j - 2)

        @pl.when(j == steps - 1)
        def _():
            finish_a(j - 1)
            finish_b(j - 1)

        @pl.when(second)
        def _():
            finish_near(j)

        @pl.when(jnp.logical_and(first, j > turnover))
        def _():
            def old(i, carry):
                finish_far(i)
                return carry

            lax.fori_loop(jnp.where(j == turnover + 1, 0, j - 1), j, old, 0)

        fwd_copy(j).wait_recv()
        relay_copy(j).start()
        normalize(slot_a, j, unit, slice(0, CHUNK), meta_a)
        relay_copy(j).wait_recv()
        normalize(slot_b, j, slot_b, part(j), meta_b, unit)
        job(own, unit[...], j, keep_pair, sent_pair, pair_copy)

        @pl.when(jnp.logical_and(first, j == turnover))
        def _():
            meta_wait_c.wait_recv()

            def ready(i, carry):
                back_copy(i).wait_recv()
                normalize(slot_c, i, slot_c, part(i), meta_c)
                return carry

            lax.fori_loop(0, steps, ready, 0)
            columns(meta_c, group_far, level_far)

        @pl.when(jnp.logical_and(first, j >= turnover))
        def _():
            def far(i, carry):
                single(i, slot_c, slot_b, part(i))
                return carry

            lax.fori_loop(jnp.where(j == turnover, 0, j), j + 1, far, 0)

        return carry

    lax.fori_loop(0, steps, main, 0)
    finish_a(steps - 1)
    a_home.start()
    finish_b(steps - 1)

    def fold(acc, count, add):
        for i in range(half // CHUNK):
            lanes = part(feat * (half // CHUNK) + i)
            for n in range(2):
                value = jnp.sum(acc[n, i * CHUNK : (i + 1) * CHUNK, :].T, axis=0, keepdims=True)
                count[n : n + 1, lanes] = value

    @pl.when(first)
    def _():
        finish_far(steps - 1)
        fold(acc_far, count_c, False)

    b_home.start()

    @pl.when(first)
    def _():
        c_home_fwd.start()

    @pl.when(second)
    def _():
        c_home_part.start()

    fold(acc_own, total, False)
    a_home.wait_recv()
    b_home.wait_recv()
    total[...] += in_a[...] + in_b[...]

    @pl.when(first)
    def _():
        c_home_fwd.wait_recv()
        c_home_part.wait_recv()
        total[...] += in_c[...] + in_d[...]

    final.start()
    final.wait_recv()
    matched = total[0:1, :] + in_f[0:1, :]
    overall = total[1:2, :] + in_f[1:2, :]
    out_ref[0:1, :] = matched
    out_ref[1:2, :] = overall - matched

    def drain(j, carry):
        fwd_copy(j).wait_send()
        relay_copy(j).wait_send()
        return carry

    lax.fori_loop(0, steps, drain, 0)
    for role, copies in (
        (side, (side_copy(1), side_copy(4))), (next_high, (row_copy(2), row_copy(5))),
        (next_low, (last_copy(2), last_copy(5))),
        (jnp.logical_and(first, high), (high_copy(0), high_copy(1), high_copy(2))),
    ):
        @pl.when(role)
        def _():
            for copy in copies:
                copy.wait_send()


    def drain_jobs(t, carry):
        job_copy(t).wait_send()
        pair_copy(t).wait_send()
        return carry

    lax.fori_loop(0, steps, drain_jobs, 0)
    for copy in (squares_copy, meta_fwd, meta_fwd_other, a_home, b_home, final):
        copy.wait_send()

    @pl.when(first)
    def _():
        def drain_c(j, carry):
            part_copy(j).wait_send()
            back_copy(j).wait_send()
            return carry

        lax.fori_loop(0, steps, drain_c, 0)
        meta_part.wait_send()
        meta_back.wait_send()
        c_home_fwd.wait_send()

    @pl.when(second)
    def _():
        c_home_part.wait_send()


def local(rows_count, features, group_index_list, threshold_codes):
    rows, width = features.shape
    full_width = width * lax.axis_size("feat")
    half = rows // 2
    steps = rows // CHUNK
    block = pltpu.VMEM((rows, width), jnp.bfloat16)
    def tiles(wide, dtype):
        return pltpu.VMEM((steps, half, wide), dtype)

    hops = steps // 2
    line = pltpu.VMEM((8, rows), F32)
    column = pltpu.VMEM((half, CHUNK), F32)
    sums = pltpu.VMEM((2, half, CHUNK), F32)
    sems = pltpu.SemaphoreType.DMA((steps,))
    vmem = pl.BlockSpec(memory_space=pltpu.VMEM)
    return pl.pallas_call(
        functools.partial(kernel, rows_count, full_width),
        out_shape=jax.ShapeDtypeStruct((2, rows), F32),
        in_specs=[pl.BlockSpec(memory_space=pl.ANY), vmem, vmem],
        out_specs=vmem,
        scratch_shapes=[
            block, block, block, block, pltpu.VMEM((hops, CHUNK, width), jnp.bfloat16),
            pltpu.VMEM((2 * CHUNK, width), jnp.bfloat16),
            *[tiles(w, t) for w in (CHUNK, 2 * CHUNK) for t in (F32, jnp.int16, jnp.int16)],
            *[line] * 6,
            *[column] * 4,
            sums, sums,
            *[line] * 9,
            *[sems] * 12,
            pltpu.SemaphoreType.DMA((10,)), pltpu.SemaphoreType.DMA((10,)),
            pltpu.SemaphoreType.DMA((hops,)), pltpu.SemaphoreType.DMA((hops,)),
        ],
        compiler_params=pltpu.CompilerParams(
            collective_id=0, has_side_effects=True, vmem_limit_bytes=56 * 1024 * 1024
        ),
    )(features, group_index_list.reshape(1, rows), threshold_codes.reshape(1, rows))


def solution(mesh):
    placed = (P("rows", "feat"), P("rows"), P("rows"))
    return jax.shard_map(
        functools.partial(local, mesh.shape["rows"]),
        mesh=mesh, in_specs=placed, out_specs=P(None, "rows"), check_vma=False,
    )
```

```python
import functools
import math

import jax
import jax.numpy as jnp
from jax import lax
from jax.experimental import pallas as pl
from jax.experimental.pallas import tpu as pltpu
from jax.sharding import PartitionSpec as P

CHUNK = 128
SCALE = math.log2(math.e) / 0.02
MESH = pl.DeviceIdType.MESH
PLANE = 16
GRID = 32000.0
F32 = jnp.float32


def turn(row):
    return jnp.broadcast_to(row, (CHUNK, CHUNK)).T


def kernel(
    rows_count, full_width,
    x_hbm, group_ref, code_ref, out_ref,
    own, slot_a, slot_b, slot_c, hop, unit,
    keep, sent, got, keep_pair, sent_pair, got_pair,
    squares, squares_in, meta, meta_a, meta_b, meta_c,
    group_own, level_own, group_far, level_far,
    acc_own, acc_far,
    count_a, count_b, count_c, total, in_a, in_b, in_c, in_d, in_f,
    load_sem, fwd_send, a_recv, relay_send, b_recv, back_send, part_send, c_recv,
    job_send, job_recv, pair_send, pair_recv, small_send, small_recv, hop_send, hop_recv,
):
    rows, width = own.shape
    half = rows // 2
    steps = rows // CHUNK
    turnover = steps - 2
    me = lax.axis_index("rows")
    feat = lax.axis_index("feat")
    core = lax.rem(me, 2)
    other = me + 1 - 2 * core
    fwd = lax.rem(me + 2, rows_count)
    back = lax.rem(me + rows_count - 2, rows_count)
    fwd_other = lax.rem(other + 2, rows_count)
    back_other = lax.rem(other + rows_count - 2, rows_count)
    mate = (me, 1 - feat)
    first = core == 0
    second = core == 1
    place = lax.rem(me // 2, PLANE)
    low, next_low, side, next_high, high = (place == n for n in (0, 1, PLANE - 4, PLANE - 2, PLANE - 1))
    bound = 2 * PLANE

    def shift(n):
        return (lax.rem(me + n + rows_count, rows_count), feat)

    def part(j):
        return pl.ds(pl.multiple_of(j * CHUNK, CHUNK), CHUNK)

    def remote(source, target, send, recv, where):
        return pltpu.make_async_remote_copy(
            src_ref=source, dst_ref=target, send_sem=send, recv_sem=recv,
            device_id=where, device_id_type=MESH,
        )

    by_side = {1: 0, 4: 1}
    by_row = {2: 0, 5: 1}
    straight = (0, 3)

    def leg_copy(j):
        slot = by_side[j] if j in by_side else by_row[j]
        return remote(
            x_hbm.at[part(j)], hop.at[slot], fwd_send.at[j], hop_recv.at[slot], shift(-6 if j in by_side else -2)
        )

    def side_copy(j):
        return remote(hop.at[by_side[j]], slot_a.at[part(j)], hop_send.at[by_side[j]], a_recv.at[j], shift(8))

    def row_copy(j):
        slot = by_row[j]
        return remote(hop.at[slot], hop.at[slot], hop_send.at[slot], hop_recv.at[slot], shift(6))

    def last_copy(j):
        return remote(hop.at[by_row[j]], slot_a.at[part(j)], hop_send.at[by_row[j]], a_recv.at[j], shift(-2))

    def back_leg_copy(j):
        return remote(x_hbm.at[part(j)], hop.at[j], back_send.at[j], hop_recv.at[j], shift(bound - 2))

    def high_copy(j):
        return remote(hop.at[j], slot_c.at[part(j)], hop_send.at[j], c_recv.at[j], shift(-bound))

    def send_fwd(js):
        @pl.when(jnp.logical_not(high))
        def _():
            for j in js:
                fwd_copy(j).start()

    def send_back(js):
        @pl.when(jnp.logical_and(first, low))
        def _():
            for j in js:
                (back_leg_copy(j) if j < steps // 2 else back_copy(j)).start()

        @pl.when(jnp.logical_and(first, jnp.logical_not(low)))
        def _():
            for j in js:
                back_copy(j).start()

    def pass_on(*legs):
        for arrived, copy in legs:
            arrived.wait_recv()
            copy.start()

    def load(j):
        return pltpu.make_async_copy(x_hbm.at[part(j)], own.at[part(j)], load_sem.at[j])

    def fwd_copy(j):
        return remote(x_hbm.at[part(j)], slot_a.at[part(j)], fwd_send.at[j], a_recv.at[j], (fwd, feat))

    def relay_copy(j):
        return remote(slot_a.at[part(j)], slot_b.at[part(j)], relay_send.at[j], b_recv.at[j], (other, feat))

    def back_copy(j):
        return remote(x_hbm.at[part(j)], slot_c.at[part(j)], back_send.at[j], c_recv.at[j], (back, feat))

    def part_copy(j):
        return remote(x_hbm.at[part(j)], slot_c.at[part(j)], part_send.at[j], c_recv.at[j], (other, feat))

    def job_copy(t):
        return remote(sent.at[t], got.at[t], job_send.at[t], job_recv.at[t], mate)

    def pair_copy(t):
        return remote(sent_pair.at[t], got_pair.at[t], pair_send.at[t], pair_recv.at[t], mate)

    def small(n, source, target, where):
        return remote(source, target, small_send.at[n], small_recv.at[n], where)

    squares_copy = small(0, squares, squares_in, mate)
    meta_fwd = small(1, meta, meta_a, (fwd, feat))
    meta_fwd_other = small(2, meta, meta_b, (fwd_other, feat))
    meta_back = remote(meta, meta_c, small_send.at[3], small_recv.at[3], (back, feat))
    meta_part = remote(meta, meta_c, small_send.at[4], small_recv.at[3], (other, feat))
    a_home = small(5, count_a, in_a, (back, feat))
    b_home = small(6, count_b, in_b, (back_other, feat))
    c_home_fwd = small(7, count_c, in_c, (fwd, feat))
    c_home_part = small(8, count_c, in_d, (other, feat))
    final = small(9, total, in_f, mate)

    for j in range(steps):
        load(j).start()
    barrier = pltpu.get_barrier_semaphore()
    peers = [(fwd, feat), (fwd_other, feat), (back, feat), (back_other, feat), (other, feat), mate]
    for peer in peers:
        pl.semaphore_signal(barrier, inc=1, device_id=peer, device_id_type=MESH)
    expected = len(peers)
    for role, offsets in (
        (low, (bound - 2, -8)), (side, (6, 8)), (high, (2 - bound, -6, bound, -bound)),
        (next_high, (6,)), (next_low, (-6,)),
    ):
        @pl.when(role)
        def _():
            for offset in offsets:
                pl.semaphore_signal(barrier, inc=1, device_id=shift(offset), device_id_type=MESH)

        expected += len(offsets) * role.astype(jnp.int32)
    pl.semaphore_wait(barrier, expected)

    @pl.when(high)
    def _():
        for j in by_row:
            leg_copy(j).start()
        leg_copy(1).start()

    send_fwd((0,))
    send_back((0,))

    @pl.when(first)
    def _():
        for j in range(steps):
            part_copy(j).start()

    def square(j, carry):
        load(j).wait()
        added = jnp.zeros((CHUNK, CHUNK), F32)
        for t in range(width // CHUNK):
            piece = own[part(j), t * CHUNK : (t + 1) * CHUNK].astype(F32)
            added = added + piece * piece
        squares[0:1, part(j)] = jnp.sum(added.T, axis=0, keepdims=True)
        return carry

    squares[...] = jnp.zeros_like(squares)
    lax.fori_loop(0, steps, square, 0)
    squares_copy.start()
    squares_copy.wait_recv()
    inverse = lax.rsqrt((squares[0:1, :] + squares_in[0:1, :]) / full_width + 1e-06) / math.sqrt(full_width)
    meta[...] = jnp.zeros_like(meta)
    meta[0:1, :] = inverse
    meta[1:2, :] = group_ref[...].astype(F32)
    meta[2:3, :] = jnp.exp2((0.2 + 0.15 * code_ref[...].astype(F32)) * SCALE)
    meta_fwd.start()
    meta_fwd_other.start()

    @pl.when(first)
    def _():
        meta_part.start()
        meta_back.start()

    @pl.when(high)
    def _():
        leg_copy(4).start()
        fwd_copy(straight[0]).start()

    send_fwd((1, 2, 3, 4, 5))
    send_back((1, 2, 3, 4, 5))

    def normalize(source, j, target, into, meta_ref, also=None):
        factor = turn(meta_ref[0:1, part(j)])
        for t in range(width // CHUNK):
            lanes = slice(t * CHUNK, (t + 1) * CHUNK)
            value = (source[part(j), lanes].astype(F32) * factor).astype(jnp.bfloat16)
            target[into, lanes] = value
            if also is not None:
                also[CHUNK:, lanes] = value

    def own_unit(j, carry):
        normalize(own, j, own, part(j), meta)
        return carry

    lax.fori_loop(0, steps, own_unit, 0)

    def columns(meta_ref, group_col, level_col):
        for i in range(half // CHUNK):
            lanes = part(feat * (half // CHUNK) + i)
            group_col[i * CHUNK : (i + 1) * CHUNK, :] = turn(meta_ref[1:2, lanes])
            level_col[i * CHUNK : (i + 1) * CHUNK, :] = turn(meta_ref[2:3, lanes])

    columns(meta, group_own, level_own)
    acc_own[...] = jnp.zeros_like(acc_own)
    acc_far[...] = jnp.zeros_like(acc_far)
    for ref in (count_a, count_b, count_c, total):
        ref[...] = jnp.zeros_like(ref)

    def job(fixed, chunk, t, held, outgoing, copy):
        for where, target in ((1 - feat, outgoing), (feat, held)):
            lines = pl.ds(pl.multiple_of(where * half, half), half)
            value = lax.dot_general(
                fixed[lines, :], chunk, (((1,), (1,)), ((), ())), preferred_element_type=F32
            )
            if target is outgoing:
                target[t] = jnp.round(value * GRID).astype(jnp.int32).astype(jnp.int16)
                copy(t).start()
            else:
                target[t] = value

    def single(t, fixed, moving, at):
        job(fixed, moving[at, :], t, keep, sent, job_copy)

    size = 32

    def finish(held, arrived, t, lanes, j, group_col, level_col, acc, meta_ref, count):
        group_row = jnp.broadcast_to(meta_ref[1:2, part(j)], (size, CHUNK))
        level_row = jnp.broadcast_to(meta_ref[2:3, part(j)], (size, CHUNK))

        def piece(i, carry):
            matched, overall = carry
            at = pl.ds(pl.multiple_of(i * size, size), size)
            power = jnp.exp2(held[t, at, lanes] * (-SCALE) + arrived[t, at, lanes].astype(F32) * (-SCALE / GRID))
            mine = 1.0 / (1.0 + level_col[at, :] * power)
            yours = 1.0 / (1.0 + level_row * power)
            same = group_col[at, :] == group_row
            acc[0, at, :] += jnp.where(same, mine, 0.0)
            acc[1, at, :] += mine
            return matched + jnp.where(same, yours, 0.0), overall + yours

        zero = jnp.zeros((size, CHUNK), F32)
        matched, overall = lax.fori_loop(0, half // size, piece, (zero, zero))
        count[0:1, part(j)] += jnp.sum(matched, axis=0, keepdims=True)
        count[1:2, part(j)] += jnp.sum(overall, axis=0, keepdims=True)

    every, left, right = slice(0, CHUNK), slice(0, CHUNK), slice(CHUNK, 2 * CHUNK)

    def finish_a(j):
        pair_copy(j).wait_recv()
        finish(keep_pair, got_pair, j, left, j, group_own, level_own, acc_own, meta_a, count_a)

    def finish_b(j):
        finish(keep_pair, got_pair, j, right, j, group_own, level_own, acc_own, meta_b, count_b)

    def finish_near(j):
        job_copy(j).wait_recv()
        finish(keep, got, j, every, j, group_own, level_own, acc_own, meta_c, count_c)

    def finish_far(j):
        job_copy(j).wait_recv()
        finish(keep, got, j, every, j, group_far, level_far, acc_far, meta_b, count_b)

    meta_wait_c = remote(meta, meta_c, small_send.at[3], small_recv.at[3], (back, feat))

    @pl.when(second)
    def _():
        meta_wait_c.wait_recv()

        def step(j, carry):
            part_copy(j).wait_recv()
            normalize(slot_c, j, slot_c, part(j), meta_c)
            single(j, own, slot_c, part(j))
            return carry

        lax.fori_loop(0, steps, step, 0)

    meta_fwd.wait_recv()
    meta_fwd_other.wait_recv()

    def main(j, carry):
        for turn_at, role, act in (
            (1, high, lambda: fwd_copy(straight[1]).start()),
            (0, side, lambda: pass_on((leg_copy(1), side_copy(1)))),
            (2, side, lambda: pass_on((leg_copy(4), side_copy(4)))),
            (0, next_high, lambda: pass_on((leg_copy(2), row_copy(2)))),
            (2, next_high, lambda: pass_on((leg_copy(5), row_copy(5)))),
            (3, next_low, lambda: pass_on((row_copy(2), last_copy(2)))),
            (5, next_low, lambda: pass_on((row_copy(5), last_copy(5)))),
            (1, jnp.logical_and(first, high), lambda: pass_on(*((back_leg_copy(i), high_copy(i)) for i in (0, 1)))),
            (2, jnp.logical_and(first, high), lambda: pass_on((back_leg_copy(2), high_copy(2)))),
        ):
            pl.when(jnp.logical_and(j == turn_at, role))(act)

        fwd_copy(j).wait_recv()
        relay_copy(j).start()
        normalize(slot_a, j, unit, slice(0, CHUNK), meta_a)
        relay_copy(j).wait_recv()
        normalize(slot_b, j, slot_b, part(j), meta_b, unit)
        job(own, unit[...], j, keep_pair, sent_pair, pair_copy)

        @pl.when(jnp.logical_and(first, j == turnover))
        def _():
            meta_wait_c.wait_recv()

            def ready(i, carry):
                back_copy(i).wait_recv()
                normalize(slot_c, i, slot_c, part(i), meta_c)
                return carry

            lax.fori_loop(0, steps, ready, 0)
            columns(meta_c, group_far, level_far)

        @pl.when(jnp.logical_and(first, j >= turnover))
        def _():
            def far(i, carry):
                single(i, slot_c, slot_b, part(i))
                return carry

            lax.fori_loop(jnp.where(j == turnover, 0, j), j + 1, far, 0)

        @pl.when(j > 1)
        def _():
            finish_a(j - 2)
            finish_b(j - 2)

        @pl.when(j == steps - 1)
        def _():
            finish_a(j - 1)
            finish_b(j - 1)

        @pl.when(second)
        def _():
            finish_near(j)

        @pl.when(jnp.logical_and(first, j > turnover))
        def _():
            def old(i, carry):
                finish_far(i)
                return carry

            lax.fori_loop(jnp.where(j == turnover + 1, 0, j - 1), j, old, 0)

        return carry

    lax.fori_loop(0, steps, main, 0)
    finish_a(steps - 1)
    a_home.start()
    finish_b(steps - 1)

    def fold(acc, count, add):
        for i in range(half // CHUNK):
            lanes = part(feat * (half // CHUNK) + i)
            for n in range(2):
                value = jnp.sum(acc[n, i * CHUNK : (i + 1) * CHUNK, :].T, axis=0, keepdims=True)
                count[n : n + 1, lanes] = value

    @pl.when(first)
    def _():
        finish_far(steps - 1)
        fold(acc_far, count_c, False)

    b_home.start()

    @pl.when(first)
    def _():
        c_home_fwd.start()

    @pl.when(second)
    def _():
        c_home_part.start()

    fold(acc_own, total, False)
    a_home.wait_recv()
    b_home.wait_recv()
    total[...] += in_a[...] + in_b[...]

    @pl.when(first)
    def _():
        c_home_fwd.wait_recv()
        c_home_part.wait_recv()
        total[...] += in_c[...] + in_d[...]

    final.start()
    final.wait_recv()
    matched = total[0:1, :] + in_f[0:1, :]
    overall = total[1:2, :] + in_f[1:2, :]
    out_ref[0:1, :] = matched
    out_ref[1:2, :] = overall - matched

    def drain(j, carry):
        fwd_copy(j).wait_send()
        relay_copy(j).wait_send()
        return carry

    lax.fori_loop(0, steps, drain, 0)
    for role, copies in (
        (side, (side_copy(1), side_copy(4))), (next_high, (row_copy(2), row_copy(5))),
        (next_low, (last_copy(2), last_copy(5))),
        (jnp.logical_and(first, high), (high_copy(0), high_copy(1), high_copy(2))),
    ):
        @pl.when(role)
        def _():
            for copy in copies:
                copy.wait_send()


    def drain_jobs(t, carry):
        job_copy(t).wait_send()
        pair_copy(t).wait_send()
        return carry

    lax.fori_loop(0, steps, drain_jobs, 0)
    for copy in (squares_copy, meta_fwd, meta_fwd_other, a_home, b_home, final):
        copy.wait_send()

    @pl.when(first)
    def _():
        def drain_c(j, carry):
            part_copy(j).wait_send()
            back_copy(j).wait_send()
            return carry

        lax.fori_loop(0, steps, drain_c, 0)
        meta_part.wait_send()
        meta_back.wait_send()
        c_home_fwd.wait_send()

    @pl.when(second)
    def _():
        c_home_part.wait_send()


def local(rows_count, features, group_index_list, threshold_codes):
    rows, width = features.shape
    full_width = width * lax.axis_size("feat")
    half = rows // 2
    steps = rows // CHUNK
    block = pltpu.VMEM((rows, width), jnp.bfloat16)
    def tiles(wide, dtype):
        return pltpu.VMEM((steps, half, wide), dtype)

    hops = steps // 2
    line = pltpu.VMEM((8, rows), F32)
    column = pltpu.VMEM((half, CHUNK), F32)
    sums = pltpu.VMEM((2, half, CHUNK), F32)
    sems = pltpu.SemaphoreType.DMA((steps,))
    vmem = pl.BlockSpec(memory_space=pltpu.VMEM)
    return pl.pallas_call(
        functools.partial(kernel, rows_count, full_width),
        out_shape=jax.ShapeDtypeStruct((2, rows), F32),
        in_specs=[pl.BlockSpec(memory_space=pl.ANY), vmem, vmem],
        out_specs=vmem,
        scratch_shapes=[
            block, block, block, block, pltpu.VMEM((hops, CHUNK, width), jnp.bfloat16),
            pltpu.VMEM((2 * CHUNK, width), jnp.bfloat16),
            *[tiles(w, t) for w in (CHUNK, 2 * CHUNK) for t in (F32, jnp.int16, jnp.int16)],
            *[line] * 6,
            *[column] * 4,
            sums, sums,
            *[line] * 9,
            *[sems] * 12,
            pltpu.SemaphoreType.DMA((10,)), pltpu.SemaphoreType.DMA((10,)),
            pltpu.SemaphoreType.DMA((hops,)), pltpu.SemaphoreType.DMA((hops,)),
        ],
        compiler_params=pltpu.CompilerParams(
            collective_id=0, has_side_effects=True, vmem_limit_bytes=56 * 1024 * 1024
        ),
    )(features, group_index_list.reshape(1, rows), threshold_codes.reshape(1, rows))


def solution(mesh):
    placed = (P("rows", "feat"), P("rows"), P("rows"))
    return jax.shard_map(
        functools.partial(local, mesh.shape["rows"]),
        mesh=mesh, in_specs=placed, out_specs=P(None, "rows"), check_vma=False,
    )
```

```python
import functools
import math

import jax
import jax.numpy as jnp
from jax import lax
from jax.experimental import pallas as pl
from jax.experimental.pallas import tpu as pltpu
from jax.sharding import PartitionSpec as P

CHUNK = 128
SCALE = math.log2(math.e) / 0.02
MESH = pl.DeviceIdType.MESH
PLANE = 16
GRID = 32000.0
F32 = jnp.float32


def turn(row):
    return jnp.broadcast_to(row, (CHUNK, CHUNK)).T


def kernel(
    rows_count, full_width,
    x_hbm, group_ref, code_ref, out_ref,
    own, slot_a, slot_b, slot_c, hop, unit,
    keep, sent, got, keep_pair, sent_pair, got_pair,
    squares, squares_in, meta, meta_a, meta_b, meta_c,
    group_own, level_own, group_far, level_far,
    acc_own, acc_far,
    count_a, count_b, count_c, total, in_a, in_b, in_c, in_d, in_f,
    load_sem, fwd_send, a_recv, relay_send, b_recv, back_send, part_send, c_recv,
    job_send, job_recv, pair_send, pair_recv, small_send, small_recv, hop_send, hop_recv,
):
    rows, width = own.shape
    half = rows // 2
    steps = rows // CHUNK
    turnover = steps - 2
    me = lax.axis_index("rows")
    feat = lax.axis_index("feat")
    core = lax.rem(me, 2)
    other = me + 1 - 2 * core
    fwd = lax.rem(me + 2, rows_count)
    back = lax.rem(me + rows_count - 2, rows_count)
    fwd_other = lax.rem(other + 2, rows_count)
    back_other = lax.rem(other + rows_count - 2, rows_count)
    mate = (me, 1 - feat)
    first = core == 0
    second = core == 1
    place = lax.rem(me // 2, PLANE)
    low, next_low, side, next_high, high = (place == n for n in (0, 1, PLANE - 4, PLANE - 2, PLANE - 1))
    bound = 2 * PLANE

    def shift(n):
        return (lax.rem(me + n + rows_count, rows_count), feat)

    def part(j):
        return pl.ds(pl.multiple_of(j * CHUNK, CHUNK), CHUNK)

    def remote(source, target, send, recv, where):
        return pltpu.make_async_remote_copy(
            src_ref=source, dst_ref=target, send_sem=send, recv_sem=recv,
            device_id=where, device_id_type=MESH,
        )

    by_side = {1: 0, 4: 1}
    by_row = {2: 0, 5: 1}
    straight = (0, 3)

    def leg_copy(j):
        slot = by_side[j] if j in by_side else by_row[j]
        return remote(
            x_hbm.at[part(j)], hop.at[slot], fwd_send.at[j], hop_recv.at[slot], shift(-6 if j in by_side else -2)
        )

    def side_copy(j):
        return remote(hop.at[by_side[j]], slot_a.at[part(j)], hop_send.at[by_side[j]], a_recv.at[j], shift(8))

    def row_copy(j):
        slot = by_row[j]
        return remote(hop.at[slot], hop.at[slot], hop_send.at[slot], hop_recv.at[slot], shift(6))

    def last_copy(j):
        return remote(hop.at[by_row[j]], slot_a.at[part(j)], hop_send.at[by_row[j]], a_recv.at[j], shift(-2))

    def back_leg_copy(j):
        return remote(x_hbm.at[part(j)], hop.at[j], back_send.at[j], hop_recv.at[j], shift(bound - 2))

    def high_copy(j):
        return remote(hop.at[j], slot_c.at[part(j)], hop_send.at[j], c_recv.at[j], shift(-bound))

    def send_fwd(js):
        @pl.when(jnp.logical_not(high))
        def _():
            for j in js:
                fwd_copy(j).start()

    def send_back(js):
        @pl.when(jnp.logical_and(first, low))
        def _():
            for j in js:
                (back_leg_copy(j) if j < steps // 2 else back_copy(j)).start()

        @pl.when(jnp.logical_and(first, jnp.logical_not(low)))
        def _():
            for j in js:
                back_copy(j).start()

    def pass_on(*legs):
        for arrived, copy in legs:
            arrived.wait_recv()
            copy.start()

    def load(j):
        return pltpu.make_async_copy(x_hbm.at[part(j)], own.at[part(j)], load_sem.at[j])

    def fwd_copy(j):
        return remote(x_hbm.at[part(j)], slot_a.at[part(j)], fwd_send.at[j], a_recv.at[j], (fwd, feat))

    def relay_copy(j):
        return remote(slot_a.at[part(j)], slot_b.at[part(j)], relay_send.at[j], b_recv.at[j], (other, feat))

    def back_copy(j):
        return remote(x_hbm.at[part(j)], slot_c.at[part(j)], back_send.at[j], c_recv.at[j], (back, feat))

    def part_copy(j):
        return remote(x_hbm.at[part(j)], slot_c.at[part(j)], part_send.at[j], c_recv.at[j], (other, feat))

    def job_copy(t):
        return remote(sent.at[t], got.at[t], job_send.at[t], job_recv.at[t], mate)

    def pair_copy(t):
        return remote(sent_pair.at[t], got_pair.at[t], pair_send.at[t], pair_recv.at[t], mate)

    def small(n, source, target, where):
        return remote(source, target, small_send.at[n], small_recv.at[n], where)

    squares_copy = small(0, squares, squares_in, mate)
    meta_fwd = small(1, meta, meta_a, (fwd, feat))
    meta_fwd_other = small(2, meta, meta_b, (fwd_other, feat))
    meta_back = remote(meta, meta_c, small_send.at[3], small_recv.at[3], (back, feat))
    meta_part = remote(meta, meta_c, small_send.at[4], small_recv.at[3], (other, feat))
    a_home = small(5, count_a, in_a, (back, feat))
    b_home = small(6, count_b, in_b, (back_other, feat))
    c_home_fwd = small(7, count_c, in_c, (fwd, feat))
    c_home_part = small(8, count_c, in_d, (other, feat))
    final = small(9, total, in_f, mate)

    for j in range(steps):
        load(j).start()
    barrier = pltpu.get_barrier_semaphore()
    peers = [(fwd, feat), (fwd_other, feat), (back, feat), (back_other, feat), (other, feat), mate]
    for peer in peers:
        pl.semaphore_signal(barrier, inc=1, device_id=peer, device_id_type=MESH)
    expected = len(peers)
    for role, offsets in (
        (low, (bound - 2, -8)), (side, (6, 8)), (high, (2 - bound, -6, bound, -bound)),
        (next_high, (6,)), (next_low, (-6,)),
    ):
        @pl.when(role)
        def _():
            for offset in offsets:
                pl.semaphore_signal(barrier, inc=1, device_id=shift(offset), device_id_type=MESH)

        expected += len(offsets) * role.astype(jnp.int32)
    pl.semaphore_wait(barrier, expected)

    @pl.when(high)
    def _():
        for j in by_row:
            leg_copy(j).start()
        leg_copy(1).start()

    send_fwd((0,))
    send_back((0,))

    @pl.when(first)
    def _():
        for j in range(steps):
            part_copy(j).start()

    def square(j, carry):
        load(j).wait()
        added = jnp.zeros((CHUNK, CHUNK), F32)
        for t in range(width // CHUNK):
            piece = own[part(j), t * CHUNK : (t + 1) * CHUNK].astype(F32)
            added = added + piece * piece
        squares[0:1, part(j)] = jnp.sum(added.T, axis=0, keepdims=True)
        return carry

    squares[...] = jnp.zeros_like(squares)
    lax.fori_loop(0, steps, square, 0)
    squares_copy.start()
    squares_copy.wait_recv()
    inverse = lax.rsqrt((squares[0:1, :] + squares_in[0:1, :]) / full_width + 1e-06) / math.sqrt(full_width)
    meta[...] = jnp.zeros_like(meta)
    meta[0:1, :] = inverse
    meta[1:2, :] = group_ref[...].astype(F32)
    meta[2:3, :] = jnp.exp2((0.2 + 0.15 * code_ref[...].astype(F32)) * SCALE)
    meta_fwd.start()
    meta_fwd_other.start()

    @pl.when(first)
    def _():
        meta_part.start()
        meta_back.start()

    @pl.when(high)
    def _():
        leg_copy(4).start()
        for j in straight:
            fwd_copy(j).start()

    send_fwd((1, 2, 3, 4, 5))
    send_back((1, 2, 3, 4, 5))

    def normalize(source, j, target, into, meta_ref, also=None):
        factor = turn(meta_ref[0:1, part(j)])
        for t in range(width // CHUNK):
            lanes = slice(t * CHUNK, (t + 1) * CHUNK)
            value = (source[part(j), lanes].astype(F32) * factor).astype(jnp.bfloat16)
            target[into, lanes] = value
            if also is not None:
                also[CHUNK:, lanes] = value

    def own_unit(j, carry):
        normalize(own, j, own, part(j), meta)
        return carry

    lax.fori_loop(0, steps, own_unit, 0)

    def columns(meta_ref, group_col, level_col):
        for i in range(half // CHUNK):
            lanes = part(feat * (half // CHUNK) + i)
            group_col[i * CHUNK : (i + 1) * CHUNK, :] = turn(meta_ref[1:2, lanes])
            level_col[i * CHUNK : (i + 1) * CHUNK, :] = turn(meta_ref[2:3, lanes])

    columns(meta, group_own, level_own)
    acc_own[...] = jnp.zeros_like(acc_own)
    acc_far[...] = jnp.zeros_like(acc_far)
    for ref in (count_a, count_b, count_c, total):
        ref[...] = jnp.zeros_like(ref)

    def job(fixed, chunk, t, held, outgoing, copy):
        for where, target in ((1 - feat, outgoing), (feat, held)):
            lines = pl.ds(pl.multiple_of(where * half, half), half)
            value = lax.dot_general(
                fixed[lines, :], chunk, (((1,), (1,)), ((), ())), preferred_element_type=F32
            )
            if target is outgoing:
                target[t] = jnp.round(value * GRID).astype(jnp.int32).astype(jnp.int16)
                copy(t).start()
            else:
                target[t] = value

    def single(t, fixed, moving, at):
        job(fixed, moving[at, :], t, keep, sent, job_copy)

    size = 32

    def finish(held, arrived, t, lanes, j, group_col, level_col, acc, meta_ref, count):
        group_row = jnp.broadcast_to(meta_ref[1:2, part(j)], (size, CHUNK))
        level_row = jnp.broadcast_to(meta_ref[2:3, part(j)], (size, CHUNK))

        def piece(i, carry):
            matched, overall = carry
            at = pl.ds(pl.multiple_of(i * size, size), size)
            power = jnp.exp2(held[t, at, lanes] * (-SCALE) + arrived[t, at, lanes].astype(F32) * (-SCALE / GRID))
            mine = 1.0 / (1.0 + level_col[at, :] * power)
            yours = 1.0 / (1.0 + level_row * power)
            same = group_col[at, :] == group_row
            acc[0, at, :] += jnp.where(same, mine, 0.0)
            acc[1, at, :] += mine
            return matched + jnp.where(same, yours, 0.0), overall + yours

        zero = jnp.zeros((size, CHUNK), F32)
        matched, overall = lax.fori_loop(0, half // size, piece, (zero, zero))
        count[0:1, part(j)] += jnp.sum(matched, axis=0, keepdims=True)
        count[1:2, part(j)] += jnp.sum(overall, axis=0, keepdims=True)

    every, left, right = slice(0, CHUNK), slice(0, CHUNK), slice(CHUNK, 2 * CHUNK)

    def finish_a(j):
        pair_copy(j).wait_recv()
        finish(keep_pair, got_pair, j, left, j, group_own, level_own, acc_own, meta_a, count_a)

    def finish_b(j):
        finish(keep_pair, got_pair, j, right, j, group_own, level_own, acc_own, meta_b, count_b)

    def finish_near(j):
        job_copy(j).wait_recv()
        finish(keep, got, j, every, j, group_own, level_own, acc_own, meta_c, count_c)

    def finish_far(j):
        job_copy(j).wait_recv()
        finish(keep, got, j, every, j, group_far, level_far, acc_far, meta_b, count_b)

    meta_wait_c = remote(meta, meta_c, small_send.at[3], small_recv.at[3], (back, feat))

    @pl.when(second)
    def _():
        meta_wait_c.wait_recv()

        def step(j, carry):
            part_copy(j).wait_recv()
            normalize(slot_c, j, slot_c, part(j), meta_c)
            single(j, own, slot_c, part(j))
            return carry

        lax.fori_loop(0, steps, step, 0)

    meta_fwd.wait_recv()
    meta_fwd_other.wait_recv()

    def main(j, carry):
        for turn_at, role, act in (
            (0, side, lambda: pass_on((leg_copy(1), side_copy(1)))),
            (2, side, lambda: pass_on((leg_copy(4), side_copy(4)))),
            (0, next_high, lambda: pass_on((leg_copy(2), row_copy(2)))),
            (2, next_high, lambda: pass_on((leg_copy(5), row_copy(5)))),
            (3, next_low, lambda: pass_on((row_copy(2), last_copy(2)))),
            (5, next_low, lambda: pass_on((row_copy(5), last_copy(5)))),
            (1, jnp.logical_and(first, high), lambda: pass_on(*((back_leg_copy(i), high_copy(i)) for i in (0, 1)))),
            (2, jnp.logical_and(first, high), lambda: pass_on((back_leg_copy(2), high_copy(2)))),
        ):
            pl.when(jnp.logical_and(j == turn_at, role))(act)

        fwd_copy(j).wait_recv()
        relay_copy(j).start()
        normalize(slot_a, j, unit, slice(0, CHUNK), meta_a)
        relay_copy(j).wait_recv()
        normalize(slot_b, j, slot_b, part(j), meta_b, unit)
        job(own, unit[...], j, keep_pair, sent_pair, pair_copy)

        @pl.when(jnp.logical_and(first, j == turnover))
        def _():
            meta_wait_c.wait_recv()

            def ready(i, carry):
                back_copy(i).wait_recv()
                normalize(slot_c, i, slot_c, part(i), meta_c)
                return carry

            lax.fori_loop(0, steps, ready, 0)
            columns(meta_c, group_far, level_far)

        @pl.when(jnp.logical_and(first, j >= turnover))
        def _():
            def far(i, carry):
                single(i, slot_c, slot_b, part(i))
                return carry

            lax.fori_loop(jnp.where(j == turnover, 0, j), j + 1, far, 0)

        @pl.when(j > 1)
        def _():
            finish_a(j - 2)
            finish_b(j - 2)

        @pl.when(j == steps - 1)
        def _():
            finish_a(j - 1)
            finish_b(j - 1)

        @pl.when(second)
        def _():
            finish_near(j)

        @pl.when(jnp.logical_and(first, j > turnover))
        def _():
            def old(i, carry):
                finish_far(i)
                return carry

            lax.fori_loop(jnp.where(j == turnover + 1, 0, j - 1), j, old, 0)

        return carry

    lax.fori_loop(0, steps, main, 0)
    finish_a(steps - 1)
    a_home.start()
    finish_b(steps - 1)

    def fold(acc, count, add):
        for i in range(half // CHUNK):
            lanes = part(feat * (half // CHUNK) + i)
            for n in range(2):
                value = jnp.sum(acc[n, i * CHUNK : (i + 1) * CHUNK, :].T, axis=0, keepdims=True)
                count[n : n + 1, lanes] = value

    @pl.when(first)
    def _():
        finish_far(steps - 1)
        fold(acc_far, count_c, False)

    b_home.start()

    @pl.when(first)
    def _():
        c_home_fwd.start()

    @pl.when(second)
    def _():
        c_home_part.start()

    fold(acc_own, total, False)
    a_home.wait_recv()
    b_home.wait_recv()
    total[...] += in_a[...] + in_b[...]

    @pl.when(first)
    def _():
        c_home_fwd.wait_recv()
        c_home_part.wait_recv()
        total[...] += in_c[...] + in_d[...]

    final.start()
    final.wait_recv()
    matched = total[0:1, :] + in_f[0:1, :]
    overall = total[1:2, :] + in_f[1:2, :]
    out_ref[0:1, :] = matched
    out_ref[1:2, :] = overall - matched

    def drain(j, carry):
        fwd_copy(j).wait_send()
        relay_copy(j).wait_send()
        return carry

    lax.fori_loop(0, steps, drain, 0)
    for role, copies in (
        (side, (side_copy(1), side_copy(4))), (next_high, (row_copy(2), row_copy(5))),
        (next_low, (last_copy(2), last_copy(5))),
        (jnp.logical_and(first, high), (high_copy(0), high_copy(1), high_copy(2))),
    ):
        @pl.when(role)
        def _():
            for copy in copies:
                copy.wait_send()


    def drain_jobs(t, carry):
        job_copy(t).wait_send()
        pair_copy(t).wait_send()
        return carry

    lax.fori_loop(0, steps, drain_jobs, 0)
    for copy in (squares_copy, meta_fwd, meta_fwd_other, a_home, b_home, final):
        copy.wait_send()

    @pl.when(first)
    def _():
        def drain_c(j, carry):
            part_copy(j).wait_send()
            back_copy(j).wait_send()
            return carry

        lax.fori_loop(0, steps, drain_c, 0)
        meta_part.wait_send()
        meta_back.wait_send()
        c_home_fwd.wait_send()

    @pl.when(second)
    def _():
        c_home_part.wait_send()


def local(rows_count, features, group_index_list, threshold_codes):
    rows, width = features.shape
    full_width = width * lax.axis_size("feat")
    half = rows // 2
    steps = rows // CHUNK
    block = pltpu.VMEM((rows, width), jnp.bfloat16)
    def tiles(wide, dtype):
        return pltpu.VMEM((steps, half, wide), dtype)

    hops = steps // 2
    line = pltpu.VMEM((8, rows), F32)
    column = pltpu.VMEM((half, CHUNK), F32)
    sums = pltpu.VMEM((2, half, CHUNK), F32)
    sems = pltpu.SemaphoreType.DMA((steps,))
    vmem = pl.BlockSpec(memory_space=pltpu.VMEM)
    return pl.pallas_call(
        functools.partial(kernel, rows_count, full_width),
        out_shape=jax.ShapeDtypeStruct((2, rows), F32),
        in_specs=[pl.BlockSpec(memory_space=pl.ANY), vmem, vmem],
        out_specs=vmem,
        scratch_shapes=[
            block, block, block, block, pltpu.VMEM((hops, CHUNK, width), jnp.bfloat16),
            pltpu.VMEM((2 * CHUNK, width), jnp.bfloat16),
            *[tiles(w, t) for w in (CHUNK, 2 * CHUNK) for t in (F32, jnp.int16, jnp.int16)],
            *[line] * 6,
            *[column] * 4,
            sums, sums,
            *[line] * 9,
            *[sems] * 12,
            pltpu.SemaphoreType.DMA((10,)), pltpu.SemaphoreType.DMA((10,)),
            pltpu.SemaphoreType.DMA((hops,)), pltpu.SemaphoreType.DMA((hops,)),
        ],
        compiler_params=pltpu.CompilerParams(
            collective_id=0, has_side_effects=True, vmem_limit_bytes=56 * 1024 * 1024
        ),
    )(features, group_index_list.reshape(1, rows), threshold_codes.reshape(1, rows))


def solution(mesh):
    placed = (P("rows", "feat"), P("rows"), P("rows"))
    return jax.shard_map(
        functools.partial(local, mesh.shape["rows"]),
        mesh=mesh, in_specs=placed, out_specs=P(None, "rows"), check_vma=False,
    )
```
